1024 devices in a mesh: leaf: 16 (over z_lo, core), head: 64 (over z_hi, y, x).
Axes of the slice: x: 4, y: 8, z: 16 (z_hi: 2, z_lo: 8; z = z_hi * 8 + z_lo), core: 2. Of those that a mesh axis runs over, the one named last changes fastest.
Arguments:
- leaf_query: bfloat16 [16384, 8192], P('leaf', 'head'), may hold values from -6 to 6
- leaf_keys: bfloat16 [16384, 8192], P('leaf', 'head'), may hold values from -6 to 6
- leaf_values: bfloat16 [16384, 8192], P('leaf', 'head'), may hold values from -6 to 6
- out_grad: bfloat16 [16384, 8192], P('leaf', 'head'), may hold values from -6 to 6
- leaf_len: int32 [16], P('leaf'), may hold values from 1 to 1024, 12288 in all
- branch_id: int32 [16], P('leaf'), may hold values from 0 to 1
- trunk_keys: bfloat16 [8192, 8192], P('leaf', 'head'), may hold values from -6 to 6
- trunk_values: bfloat16 [8192, 8192], P('leaf', 'head'), may hold values from -6 to 6
- branch_keys: bfloat16 [8192, 8192], P('leaf', 'head'), may hold values from -6 to 6
- branch_values: bfloat16 [8192, 8192], P('leaf', 'head'), may hold values from -6 to 6
- norm_gain: bfloat16 [8192], P('head'), may hold values from 0.099609375 to 1.8984375
Outputs:
- leaf_out: bfloat16 [16384, 8192], P('leaf', 'head')
- query_grad: bfloat16 [16384, 8192], P('leaf', 'head')
- key_grad: bfloat16 [16384, 8192], P('leaf', 'head')
- value_grad: bfloat16 [16384, 8192], P('leaf', 'head')
- trunk_key_grad: bfloat16 [8192, 8192], P('leaf', 'head')
- trunk_value_grad: bfloat16 [8192, 8192], P('leaf', 'head')
- branch_key_grad: bfloat16 [8192, 8192], P('leaf', 'head')
- branch_value_grad: bfloat16 [8192, 8192], P('leaf', 'head')
The draws below stay inside these ranges and needn't reach their ends.
Inputs may be any that keep to these rules, and one draw needn't show every extreme that they name: `leaf_len`: A leaf's live slots are its first ones; the longest leaf has exactly 1024.
All inputs are finite; a program needn't handle non-finite values. No bound on the sum of `leaf_len` on one device may be relied on, other than what follows from the above.
Results may differ from the reference program's by a relative error of at most 0.0058.
Values sent between devices are 32-bit elements; how exact they have to be, the bound alone decides.
No kernel may reach another device: no remote copies, remote signals or barrier semaphores. Data moves between devices by JAX's collectives and lax.ppermute only.
A program may use at most 32 MiB of HBM per device.

```python
import math
import jax
import jax.numpy as jnp
import numpy as np
from jax import lax

DH = 128
LEAF = 1024
BLOCK = 512
H = 64
TRUNK = 8192
BRANCHES = 8192
LEAVES = 16384
N_LEAF = 16


def set_ends(drawn, stream_key, low, high):
    longest = drawn.shape.index(max(drawn.shape))
    spots = []
    for shift in (0, 1):
        where = [jax.random.randint(jax.random.fold_in(stream_key, axis), (), 0, length) for axis, length in enumerate(drawn.shape)]
        where[longest] = (where[longest] + shift) % drawn.shape[longest]
        spots.append(tuple(where))
    return drawn.at[spots[0]].set(low).at[spots[1]].set(high)


def block_scale(stream_key, extent, split, least, top_value):
    loudness, own = 1.0, jax.random.fold_in(stream_key, 6)
    for axis_at, blocks in split:
        steps = jnp.exp(jax.random.uniform(jax.random.fold_in(own, axis_at), (blocks,), jnp.float32, least / len(split), top_value / len(split)))
        loudness = loudness * jnp.repeat(steps, extent[axis_at] // blocks).reshape([-1 if axis == axis_at else 1 for axis in range(len(extent))])
    return loudness


def profile(count, total, limit, skew):
    portions = [(1 << 20) // math.isqrt(grade ** skew) + 1 for grade in range(2, count + 1)]
    spare, counts = total - limit - (count - 1), [1] * (count - 1)
    while spare > 0:
        free = [i for i in range(count - 1) if counts[i] < limit]
        whole, budget = sum([portions[i] for i in free]), spare
        for i in free:
            more = min(limit - counts[i], max(1, budget * portions[i] // whole), spare)
            counts[i] = counts[i] + more
            spare = spare - more
    return np.array([limit] + counts)


def uneven_parts(rng, count, total, reach, skew):
    if count == 2:
        one = jax.random.randint(rng, (), max(1, total - reach), min(reach, total - 1) + 1)
        return jnp.stack([one, total - one])
    lengths = jnp.asarray(profile(count, total, reach, skew), jnp.int32)
    couples = (count - 1) // 2
    donor, sink = lengths[1:1 + 2 * couples:2], lengths[2:2 + 2 * couples:2]
    margin = jnp.minimum(donor - 1, reach - sink)
    moved = jax.random.randint(jax.random.fold_in(rng, 1), (couples,), 0, 1 << 20) % (margin + 1)
    lengths = lengths.at[1:1 + 2 * couples:2].set(donor - moved).at[2:2 + 2 * couples:2].set(sink + moved)
    return lengths[jax.random.permutation(jax.random.fold_in(rng, 2), count)]


def gaussian(stream_key, dims, deviation, reach, pieces=(), held_as=jnp.bfloat16):
    level = block_scale(stream_key, dims, pieces, -0.22, 0.18) if pieces else 1.0
    entries = jax.random.normal(stream_key, dims, jnp.float32) * deviation * level
    return jnp.minimum(jnp.maximum(entries, -reach), reach).astype(held_as)


def setup_inputs(seed: int = 0) -> dict:
    keys = jax.random.split(jax.random.key(seed), 12)
    leaf_query = gaussian(keys[0], (LEAVES, H * DH), 1.0, 6.0, ((0, 16), (1, 64)))
    leaf_keys = gaussian(keys[1], (LEAVES, H * DH), 1.0, 6.0, ((0, 16), (1, 64)))
    leaf_values = gaussian(keys[2], (LEAVES, H * DH), 1.0, 6.0, ((0, 16), (1, 64)))
    out_grad = gaussian(keys[3], (LEAVES, H * DH), 1.0, 6.0, ((0, 16), (1, 64)))
    leaf_len = uneven_parts(keys[4], N_LEAF, N_LEAF * LEAF * 3 // 4, LEAF, 1).astype(jnp.int32)
    branch_id = set_ends(jax.random.randint(keys[5], (N_LEAF,), 0, 2), jax.random.fold_in(keys[5], 1), 0, 1).astype(jnp.int32)
    trunk_keys = gaussian(keys[6], (TRUNK, H * DH), 1.0, 6.0, ((0, 16), (1, 64)))
    trunk_values = gaussian(keys[7], (TRUNK, H * DH), 1.0, 6.0, ((0, 16), (1, 64)))
    branch_keys = gaussian(keys[8], (BRANCHES, H * DH), 1.0, 6.0, ((0, 16), (1, 64)))
    branch_values = gaussian(keys[9], (BRANCHES, H * DH), 1.0, 6.0, ((0, 16), (1, 64)))
    norm_gain = jnp.clip(1.0 + 0.18 * jax.random.normal(keys[10], (H * DH,), jnp.float32), 0.099609375, 1.8984375).astype(jnp.bfloat16)
    return {"leaf_query": leaf_query, "leaf_keys": leaf_keys, "leaf_values": leaf_values, "out_grad": out_grad, "leaf_len": leaf_len, "branch_id": branch_id, "trunk_keys": trunk_keys, "trunk_values": trunk_values, "branch_keys": branch_keys, "branch_values": branch_values, "norm_gain": norm_gain}


epsilon = 1e-06
highest = lax.Precision.HIGHEST

def to_float(values):
    return values.astype(jnp.float32)

def rounded(values):
    return to_float(lax.optimization_barrier(values.astype(jnp.bfloat16)))

def leaf_pass(leaf_items, trunk_state, branch_state, norm_gain):
    leaf_query, leaf_keys, leaf_values, out_grad, length, branch = leaf_items
    row_count, row_width = leaf_query.shape
    head_count = row_width // DH
    block_count = row_count // BLOCK
    live_rows = (jnp.arange(row_count, dtype=jnp.int32) < length).astype(jnp.float32)
    keep_mask = live_rows.astype(jnp.bfloat16)[:, None]
    first_branch = (branch == 0).astype(jnp.float32)
    prefix_state = trunk_state + (first_branch * branch_state[0] + (1.0 - first_branch) * branch_state[1])

    def to_blocks(values):
        return to_float(values).reshape(block_count, BLOCK, head_count, DH)
    queries = to_blocks(leaf_query)
    keys_masked = to_blocks(leaf_keys * keep_mask)
    values_masked = to_blocks(leaf_values * keep_mask)
    block_sums = jnp.einsum('jthd,jthe->jhde', keys_masked, values_masked, precision=highest)
    earlier = jnp.concatenate([jnp.zeros_like(block_sums[:1]), jnp.cumsum(block_sums, axis=0)[:-1]], axis=0)
    states = rounded(prefix_state[None] + earlier)
    causal = jnp.tril(jnp.ones((BLOCK, BLOCK), jnp.float32))
    mixing = rounded(jnp.einsum('jqhd,jkhd->jhqk', queries, keys_masked, precision=highest) * causal)
    raw_out = jnp.einsum('jqhd,jhde->jqhe', queries, states, precision=highest) + jnp.einsum('jhqk,jkhe->jqhe', mixing, values_masked, precision=highest)
    raw_out = raw_out.reshape(row_count, row_width) * live_rows[:, None]
    square_sum = lax.optimization_barrier(jnp.sum(raw_out * raw_out, axis=1))
    norm_scale = lax.rsqrt(square_sum / row_width + epsilon)
    gain_values = to_float(norm_gain)
    leaf_out = (raw_out * norm_scale[:, None] * gain_values).astype(jnp.bfloat16)
    scaled_grad = to_float(out_grad) * gain_values
    inner_sum = lax.optimization_barrier(jnp.sum(raw_out * scaled_grad, axis=1))
    raw_grad = (norm_scale[:, None] * scaled_grad - raw_out * (norm_scale ** 3 * inner_sum / row_width)[:, None]) * live_rows[:, None]
    raw_grad = rounded(raw_grad).reshape(block_count, BLOCK, head_count, DH)
    prob_grad = rounded(jnp.einsum('jqhe,jkhe->jhqk', raw_grad, values_masked, precision=highest) * causal)
    query_grad = jnp.einsum('jqhe,jhde->jqhd', raw_grad, states, precision=highest) + jnp.einsum('jhqk,jkhd->jqhd', prob_grad, keys_masked, precision=highest)
    block_grads = jnp.einsum('jqhd,jqhe->jhde', queries, raw_grad, precision=highest)
    reverse_sums = jnp.cumsum(block_grads[::-1], axis=0)[::-1]
    later_sums = rounded(jnp.concatenate([reverse_sums[1:], jnp.zeros_like(block_grads[:1])], axis=0))
    key_grad = jnp.einsum('jhqk,jqhd->jkhd', prob_grad, queries, precision=highest) + jnp.einsum('jkhe,jhde->jkhd', values_masked, later_sums, precision=highest)
    value_grad = jnp.einsum('jhqk,jqhe->jkhe', mixing, raw_grad, precision=highest) + jnp.einsum('jkhd,jhde->jkhe', keys_masked, later_sums, precision=highest)
    prefix_grad = lax.optimization_barrier(jnp.sum(block_grads, axis=0))
    return (leaf_out, query_grad.reshape(row_count, row_width).astype(jnp.bfloat16), key_grad.reshape(row_count, row_width).astype(jnp.bfloat16), value_grad.reshape(row_count, row_width).astype(jnp.bfloat16), prefix_grad)

def reference(leaf_query, leaf_keys, leaf_values, out_grad, leaf_len, branch_id, trunk_keys, trunk_values, branch_keys, branch_values, norm_gain):
    row_width = H * DH
    trunk_k = to_float(trunk_keys).reshape(-1, H, DH)
    trunk_v = to_float(trunk_values).reshape(-1, H, DH)
    branch_k = to_float(branch_keys).reshape(2, -1, H, DH)
    branch_v = to_float(branch_values).reshape(2, -1, H, DH)
    trunk_state = jnp.einsum('thd,the->hde', trunk_k, trunk_v, precision=highest)
    branch_state = jnp.einsum('bthd,bthe->bhde', branch_k, branch_v, precision=highest)

    def per_leaf(leaf_items):
        return leaf_pass(leaf_items, trunk_state, branch_state, norm_gain)

    def stacked(values):
        return values.reshape(N_LEAF, LEAF, row_width)
    leaf_out, query_grad, key_grad, value_grad, prefix_grads = lax.map(per_leaf, (stacked(leaf_query), stacked(leaf_keys), stacked(leaf_values), stacked(out_grad), leaf_len, branch_id))
    first_branch = (branch_id == 0).astype(jnp.float32)[:, None, None, None]
    trunk_grad = lax.optimization_barrier(jnp.sum(prefix_grads, axis=0))
    branch_grad = jnp.stack([lax.optimization_barrier(jnp.sum(first_branch * prefix_grads, axis=0)), lax.optimization_barrier(jnp.sum((1.0 - first_branch) * prefix_grads, axis=0))])
    trunk_key_grad = jnp.einsum('the,hde->thd', trunk_v, trunk_grad, precision=highest)
    trunk_value_grad = jnp.einsum('thd,hde->the', trunk_k, trunk_grad, precision=highest)
    branch_key_grad = jnp.einsum('bthe,bhde->bthd', branch_v, branch_grad, precision=highest)
    branch_value_grad = jnp.einsum('bthd,bhde->bthe', branch_k, branch_grad, precision=highest)
    return (leaf_out.reshape(-1, row_width), query_grad.reshape(-1, row_width), key_grad.reshape(-1, row_width), value_grad.reshape(-1, row_width), trunk_key_grad.reshape(-1, row_width).astype(jnp.bfloat16), trunk_value_grad.reshape(-1, row_width).astype(jnp.bfloat16), branch_key_grad.reshape(-1, row_width).astype(jnp.bfloat16), branch_value_grad.reshape(-1, row_width).astype(jnp.bfloat16))
```

```python
import functools

import jax
import jax.numpy as jnp
from jax import lax
from jax.experimental import pallas as pl
from jax.experimental.pallas import tpu as pltpu
from jax.sharding import PartitionSpec as P

DH = 128
BLOCK = 512
EPSILON = 1e-06
F32 = jnp.float32
BF16 = jnp.bfloat16
MIB = 1 << 20

VM = pl.BlockSpec(memory_space=pltpu.VMEM)
SM = pl.BlockSpec(memory_space=pltpu.SMEM)


def dot(a, b, ca=1, cb=0):
    return lax.dot_general(a, b, (((ca,), (cb,)), ((), ())), preferred_element_type=F32)


def call(body, name, shapes, specs, flops=1000000, moved=1000000, limit=24):
    return pl.pallas_call(
        body,
        out_shape=[jax.ShapeDtypeStruct(s, d) for s, d in shapes],
        in_specs=specs,
        out_specs=[VM] * len(shapes),
        name=name,
        compiler_params=pltpu.CompilerParams(vmem_limit_bytes=limit * MIB),
        cost_estimate=pl.CostEstimate(flops=flops, bytes_accessed=moved, transcendentals=0),
    )


def chunked(ref, value, start, parts):
    rows = value.shape[0] // parts
    for part in range(parts):
        ref[part, start : start + rows, :] = value[part * rows : (part + 1) * rows]


def state_kernel(parts, branch_ref, tk_ref, tv_ref, bk_ref, bv_ref, out_ref):
    trunk = dot(tk_ref[...], tv_ref[...], 0, 0)
    branch = dot(bk_ref[...], bv_ref[...], 0, 0)
    rows = DH // parts
    chunked(out_ref, trunk, 0, parts)
    chunked(out_ref, branch, rows, parts)
    flag = jnp.full((8, DH), branch_ref[0], jnp.int32).astype(F32)
    for part in range(parts):
        out_ref[part, 2 * rows : 2 * rows + 8, :] = flag


def local_kernel(len_ref, q_ref, k_ref, v_ref, g_ref, gain_ref, qt_ref, km_ref, vm_ref, vt_ref, pt_ref, lt_ref, sgt_ref, first_ref):
    rows = q_ref.shape[0]
    keep = lax.broadcasted_iota(jnp.int32, (rows, DH), 0) < len_ref[0]
    km = jnp.where(keep, k_ref[...].astype(F32), 0.0).astype(BF16)
    vf = jnp.where(keep, v_ref[...].astype(F32), 0.0)
    vm = vf.astype(BF16)
    km_ref[...] = km
    vm_ref[...] = vm
    qt = q_ref[...].astype(F32).T.astype(BF16)
    vt = vf.T.astype(BF16)
    qt_ref[...] = qt
    vt_ref[...] = vt
    causal = lax.broadcasted_iota(jnp.int32, (BLOCK, BLOCK), 0) <= lax.broadcasted_iota(
        jnp.int32, (BLOCK, BLOCK), 1
    )
    for j in range(rows // BLOCK):
        s = slice(j * BLOCK, (j + 1) * BLOCK)
        pt = jnp.where(causal, dot(km[s], qt[:, s]), 0.0).astype(BF16)
        pt_ref[s, :] = pt
        lt_ref[:, s] = dot(vt[:, s], pt)
    for j in range(rows // BLOCK - 1):
        s = slice(j * BLOCK, (j + 1) * BLOCK)
        first_ref[j] = dot(km[s], vm[s], 0, 0)
    sgt_ref[...] = (g_ref[...].astype(F32) * gain_ref[...].astype(F32)).T


def half_sum_kernel(rows, in_ref, out_ref):
    total = in_ref[0, : 2 * rows, :]
    for part in range(1, in_ref.shape[0]):
        total = total + in_ref[part, : 2 * rows, :]
    out_ref[...] = total


def prefix_kernel(rows, members, own_ref, other_ref, flags_ref, out_ref):
    half = (lax.axis_index("leaf") // members).astype(F32)
    trunk = own_ref[:rows] + other_ref[:rows]
    mine = trunk + own_ref[rows:]
    others = trunk + other_ref[rows:]
    for part in range(members):
        flag = flags_ref[part, 2 * rows : 2 * rows + 1, :]
        out_ref[part] = jnp.where(flag == half, mine, others)


def raw_kernel(copies, len_ref, state_ref, first_ref, qt_ref, lt_ref, sgt_ref, states_ref, rawt_ref, out_ref):
    rows = qt_ref.shape[1]
    state = state_ref[...].reshape(DH, DH)
    earlier = None
    for j in range(rows // BLOCK):
        s = slice(j * BLOCK, (j + 1) * BLOCK)
        if j:
            earlier = first_ref[j - 1] if earlier is None else earlier + first_ref[j - 1]
        now = (state if earlier is None else state + earlier).astype(BF16)
        states_ref[j] = now
        keep = j * BLOCK + lax.broadcasted_iota(jnp.int32, (1, BLOCK), 1) < len_ref[0]
        raw = jnp.where(keep, dot(now, qt_ref[:, s], 0, 0) + lt_ref[:, s], 0.0)
        rawt_ref[:, s] = raw
        square = jnp.sum(raw * raw, axis=0, keepdims=True)
        inner = jnp.sum(raw * sgt_ref[:, s], axis=0, keepdims=True)
        for copy in range(copies):
            out_ref[copy, 0:1, s] = square
            out_ref[copy, 1:2, s] = inner


def spread_kernel(in_ref, out_ref):
    total = in_ref[0]
    for part in range(1, in_ref.shape[0]):
        total = total + in_ref[part]
    for copy in range(out_ref.shape[0]):
        out_ref[copy] = total


def grad_kernel(features, parts, len_ref, sums_ref, rawt_ref, sgt_ref, qt_ref, rgt_ref, norm_ref, later_ref, out_ref):
    rows = qt_ref.shape[1]
    total = sums_ref[0]
    for part in range(1, sums_ref.shape[0]):
        total = total + sums_ref[part]
    norm = lax.rsqrt(total[0:1] * (1.0 / features) + EPSILON)
    coef = norm * norm * norm * total[1:2] * (1.0 / features)
    norm_ref[...] = norm
    whole = None
    for j in reversed(range(rows // BLOCK)):
        s = slice(j * BLOCK, (j + 1) * BLOCK)
        keep = j * BLOCK + lax.broadcasted_iota(jnp.int32, (1, BLOCK), 1) < len_ref[0]
        rg = jnp.where(keep, norm[:, s] * sgt_ref[:, s] - rawt_ref[:, s] * coef[:, s], 0.0).astype(BF16)
        rgt_ref[:, s] = rg
        later_ref[j] = (jnp.zeros((DH, DH), F32) if whole is None else whole).astype(BF16)
        block = dot(qt_ref[:, s], rg, 1, 1)
        whole = block if whole is None else whole + block
    chunked(out_ref, whole, 0, parts)


def leaf_kernel(q_ref, km_ref, vm_ref, vt_ref, pt_ref, rgt_ref, states_ref, later_ref, rawt_ref, norm_ref, gain_ref, lo_ref, qg_ref, kg_ref, vg_ref):
    rows = q_ref.shape[0]
    lo_ref[...] = ((rawt_ref[...] * norm_ref[...]).T * gain_ref[...].astype(F32)).astype(BF16)
    first = lax.broadcasted_iota(jnp.int32, (BLOCK, BLOCK), 0)
    second = lax.broadcasted_iota(jnp.int32, (BLOCK, BLOCK), 1)
    for j in range(rows // BLOCK):
        s = slice(j * BLOCK, (j + 1) * BLOCK)
        rgt = rgt_ref[:, s]
        rg = rgt.astype(F32).T.astype(BF16)
        dp = jnp.where(second <= first, dot(rg, vt_ref[:, s]), 0.0).astype(BF16)
        qg_ref[s, :] = (dot(rg, states_ref[j], 1, 1) + dot(dp, km_ref[s, :])).astype(BF16)
        dpt = jnp.where(first <= second, dot(vm_ref[s, :], rgt), 0.0).astype(BF16)
        kg_ref[s, :] = (dot(dpt, q_ref[s, :]) + dot(vm_ref[s, :], later_ref[j], 1, 1)).astype(BF16)
        vg_ref[s, :] = (dot(pt_ref[s, :], rg) + dot(km_ref[s, :], later_ref[j])).astype(BF16)


def by_branch_kernel(rows, in_ref, flags_ref, out_ref):
    zero = one = None
    for part in range(in_ref.shape[0]):
        value = in_ref[part]
        first = flags_ref[part, 2 * rows : 2 * rows + 1, :] == 0.0
        a = jnp.where(first, value, 0.0)
        b = jnp.where(first, 0.0, value)
        zero = a if zero is None else zero + a
        one = b if one is None else one + b
    out_ref[:rows] = zero
    out_ref[rows:] = one


def total_kernel(rows, members, own_ref, other_ref, out_ref):
    zero = own_ref[:rows] + other_ref[:rows]
    one = own_ref[rows:] + other_ref[rows:]
    own = jnp.where(lax.axis_index("leaf") >= members, one, zero)
    both = zero + one
    for part in range(members):
        out_ref[part, :rows] = both
        out_ref[part, rows:] = own


def tree_kernel(rows, in_ref, tk_ref, tv_ref, bk_ref, bv_ref, tkg_ref, tvg_ref, bkg_ref, bvg_ref):
    for start, k_ref, v_ref, kg_ref, vg_ref in (
        (0, tk_ref, tv_ref, tkg_ref, tvg_ref),
        (rows, bk_ref, bv_ref, bkg_ref, bvg_ref),
    ):
        grad = in_ref[:, start : start + rows, :].reshape(DH, DH)
        high = grad.astype(BF16)
        rest = grad - high.astype(F32)
        middle = rest.astype(BF16)
        low = (rest - middle.astype(F32)).astype(BF16)
        keys, values = k_ref[...], v_ref[...]
        kg_ref[...] = (dot(values, high, 1, 1) + (dot(values, middle, 1, 1) + dot(values, low, 1, 1))).astype(BF16)
        vg_ref[...] = (dot(keys, high) + (dot(keys, middle) + dot(keys, low))).astype(BF16)


def shards(mesh_shape, leaf_query, leaf_keys, leaf_values, out_grad, leaf_len, branch_id, trunk_keys, trunk_values, branch_keys, branch_values, norm_gain):
    leaves, heads = mesh_shape
    rows = leaf_query.shape[0]
    tree_rows = trunk_keys.shape[0]
    blocks = rows // BLOCK
    members = leaves // 2
    part = DH // members
    halves = [[h * members + i for i in range(members)] for h in range(2)]
    near = 4
    far = heads // near
    near_groups = [[g * near + i for i in range(near)] for g in range(far)]
    far_groups = [[i + near * g for g in range(far)] for i in range(near)]
    across = [(i, i ^ members) for i in range(leaves)]
    gain = norm_gain.reshape(1, DH)

    def exchange(value, axis, groups):
        return lax.all_to_all(value, axis, 0, 0, tiled=True, axis_index_groups=groups)

    (sent,) = call(functools.partial(state_kernel, members), "state", [((members, 2 * part + 8, DH), F32)], [SM] + [VM] * 4)(
        branch_id, trunk_keys, trunk_values, branch_keys, branch_values
    )
    got = exchange(sent, "leaf", halves)
    qt, km, vm, vt, pt, lt, sgt, first = call(
        local_kernel,
        "local",
        [
            ((DH, rows), BF16),
            ((rows, DH), BF16),
            ((rows, DH), BF16),
            ((DH, rows), BF16),
            ((rows, BLOCK), BF16),
            ((DH, rows), F32),
            ((DH, rows), F32),
            ((blocks - 1, DH, DH), F32),
        ],
        [SM] + [VM] * 5,
        flops=4 * rows * BLOCK * DH,
        moved=6 * MIB,
    )(leaf_len, leaf_query, leaf_keys, leaf_values, out_grad, gain)
    (half,) = call(functools.partial(half_sum_kernel, part), "half", [((2 * part, DH), F32)], [VM])(got)
    other = lax.ppermute(half, "leaf", across)
    (chunk,) = call(functools.partial(prefix_kernel, part, members), "prefix", [((members, part, DH), F32)], [VM] * 3)(half, other, got)
    state = exchange(chunk, "leaf", halves)
    states, rawt, sums = call(
        functools.partial(raw_kernel, near),
        "raw",
        [((blocks, DH, DH), BF16), ((DH, rows), F32), ((near, 2, rows), F32)],
        [SM] + [VM] * 5,
    )(leaf_len, state, first, qt, lt, sgt)
    sums = exchange(sums, "head", near_groups)
    (sums,) = call(spread_kernel, "spread", [((far, 2, rows), F32)], [VM])(sums)
    sums = exchange(sums, "head", far_groups)
    rgt, norm, later, sent = call(
        functools.partial(grad_kernel, heads * DH, members),
        "grad",
        [((DH, rows), BF16), ((1, rows), F32), ((blocks, DH, DH), BF16), ((members, part, DH), F32)],
        [SM] + [VM] * 4,
    )(leaf_len, sums, rawt, sgt, qt)
    parts = exchange(sent, "leaf", halves)
    leaf = ((rows, DH), BF16)
    leaf_grads = call(
        leaf_kernel, "leaf", [leaf] * 4, [VM] * 11, flops=8 * rows * BLOCK * DH, moved=6 * MIB
    )(leaf_query, km, vm, vt, pt, rgt, states, later, rawt, norm, gain)
    (own,) = call(functools.partial(by_branch_kernel, part), "by_branch", [((2 * part, DH), F32)], [VM] * 2)(parts, got)
    other = lax.ppermute(own, "leaf", across)
    (sent,) = call(functools.partial(total_kernel, part, members), "total", [((members, 2 * part, DH), F32)], [VM] * 2)(own, other)
    grads = exchange(sent, "leaf", halves)
    tree = ((tree_rows, DH), BF16)
    tree_grads = call(functools.partial(tree_kernel, part), "tree", [tree] * 4, [VM] * 5)(
        grads, trunk_keys, trunk_values, branch_keys, branch_values
    )
    return (*leaf_grads, *tree_grads)


def solution(mesh):
    wide = P("leaf", "head")
    placed = (wide, wide, wide, wide, P("leaf"), P("leaf"), wide, wide, wide, wide, P("head"))
    return jax.shard_map(
        functools.partial(shards, (mesh.shape["leaf"], mesh.shape["head"])),
        mesh=mesh,
        in_specs=placed,
        out_specs=(wide,) * 8,
        check_vma=False,
    )
```

```python
import functools

import jax
import jax.numpy as jnp
from jax import lax
from jax.experimental import pallas as pl
from jax.experimental.pallas import tpu as pltpu
from jax.sharding import PartitionSpec as P

DH = 128
BLOCK = 512
EPSILON = 1e-06
F32 = jnp.float32
BF16 = jnp.bfloat16
MIB = 1 << 20

VM = pl.BlockSpec(memory_space=pltpu.VMEM)
SM = pl.BlockSpec(memory_space=pltpu.SMEM)
HB = pl.BlockSpec(memory_space=pltpu.MemorySpace.HBM)
ANY = pl.BlockSpec(memory_space=pl.ANY)


def dot(a, b, ca=1, cb=0):
    return lax.dot_general(a, b, (((ca,), (cb,)), ((), ())), preferred_element_type=F32)


def call(body, name, shapes, specs, flops=1000000, moved=1000000, limit=24, out=None, scratch=()):
    return pl.pallas_call(
        body,
        out_shape=[jax.ShapeDtypeStruct(s, d) for s, d in shapes],
        in_specs=specs,
        out_specs=out or [VM] * len(shapes),
        scratch_shapes=list(scratch),
        name=name,
        compiler_params=pltpu.CompilerParams(vmem_limit_bytes=limit * MIB),
        cost_estimate=pl.CostEstimate(flops=flops, bytes_accessed=moved, transcendentals=0),
    )


def chunked(ref, value, start, parts):
    rows = value.shape[0] // parts
    for part in range(parts):
        ref[part, start : start + rows, :] = value[part * rows : (part + 1) * rows]


def state_kernel(parts, len_ref, branch_ref, tk_hbm, tv_hbm, bk_hbm, bv_hbm, out_ref, tk_ref, tv_ref, bk_ref, bv_ref, sems):
    copies = [
        pltpu.make_async_copy(source, target, sems.at[i])
        for i, (source, target) in enumerate(
            ((tk_hbm, tk_ref), (tv_hbm, tv_ref), (bk_hbm, bk_ref), (bv_hbm, bv_ref))
        )
    ]
    for copy in copies:
        copy.start()
    rows = DH // parts
    copies[0].wait()
    copies[1].wait()
    chunked(out_ref, dot(tk_ref[...], tv_ref[...], 0, 0), 0, parts)
    copies[2].wait()
    copies[3].wait()
    chunked(out_ref, dot(bk_ref[...], bv_ref[...], 0, 0), rows, parts)
    flag = jnp.full((8, DH), branch_ref[0], jnp.int32).astype(F32)
    for part in range(parts):
        out_ref[part, 2 * rows : 2 * rows + 8, :] = flag


def local_kernel(len_ref, q_ref, k_ref, v_ref, g_ref, gain_ref, after_ref, qt_ref, km_ref, vm_ref, vt_ref, pt_ref, lt_ref, sgt_ref, first_ref):
    rows = q_ref.shape[0]
    keep = lax.broadcasted_iota(jnp.int32, (rows, DH), 0) < len_ref[0]
    km = jnp.where(keep, k_ref[...].astype(F32), 0.0).astype(BF16)
    vf = jnp.where(keep, v_ref[...].astype(F32), 0.0)
    vm = vf.astype(BF16)
    km_ref[...] = km
    vm_ref[...] = vm
    qt = q_ref[...].astype(F32).T.astype(BF16)
    vt = vf.T.astype(BF16)
    qt_ref[...] = qt
    vt_ref[...] = vt
    causal = lax.broadcasted_iota(jnp.int32, (BLOCK, BLOCK), 0) <= lax.broadcasted_iota(
        jnp.int32, (BLOCK, BLOCK), 1
    )
    for j in range(rows // BLOCK):
        s = slice(j * BLOCK, (j + 1) * BLOCK)
        pt = jnp.where(causal, dot(km[s], qt[:, s]), 0.0).astype(BF16)
        pt_ref[s, :] = pt
        lt_ref[:, s] = dot(vt[:, s], pt)
    for j in range(rows // BLOCK - 1):
        s = slice(j * BLOCK, (j + 1) * BLOCK)
        first_ref[j] = dot(km[s], vm[s], 0, 0)
    sgt_ref[...] = (g_ref[...].astype(F32) * gain_ref[...].astype(F32)).T


def half_sum_kernel(rows, in_ref, out_ref):
    total = in_ref[0, : 2 * rows, :]
    for part in range(1, in_ref.shape[0]):
        total = total + in_ref[part, : 2 * rows, :]
    out_ref[...] = total


def prefix_kernel(rows, members, own_ref, other_ref, flags_ref, after_ref, out_ref):
    half = (lax.axis_index("leaf") // members).astype(F32)
    trunk = own_ref[:rows] + other_ref[:rows]
    mine = trunk + own_ref[rows:]
    others = trunk + other_ref[rows:]
    for part in range(members):
        flag = flags_ref[part, 2 * rows : 2 * rows + 1, :]
        out_ref[part] = jnp.where(flag == half, mine, others)


def raw_kernel(copies, len_ref, state_ref, first_ref, qt_ref, lt_ref, sgt_ref, states_ref, rawt_ref, out_ref):
    rows = qt_ref.shape[1]
    state = state_ref[...].reshape(DH, DH)
    earlier = None
    for j in range(rows // BLOCK):
        s = slice(j * BLOCK, (j + 1) * BLOCK)
        if j:
            earlier = first_ref[j - 1] if earlier is None else earlier + first_ref[j - 1]
        now = (state if earlier is None else state + earlier).astype(BF16)
        states_ref[j] = now
        keep = j * BLOCK + lax.broadcasted_iota(jnp.int32, (1, BLOCK), 1) < len_ref[0]
        raw = jnp.where(keep, dot(now, qt_ref[:, s], 0, 0) + lt_ref[:, s], 0.0)
        rawt_ref[:, s] = raw
        square = jnp.sum(raw * raw, axis=0, keepdims=True)
        inner = jnp.sum(raw * sgt_ref[:, s], axis=0, keepdims=True)
        for copy in range(copies):
            out_ref[copy, 0:1, s] = square
            out_ref[copy, 1:2, s] = inner


def spread_kernel(in_ref, out_ref):
    total = in_ref[0]
    for part in range(1, in_ref.shape[0]):
        total = total + in_ref[part]
    for copy in range(out_ref.shape[0]):
        out_ref[copy] = total


def grad_kernel(features, parts, len_ref, sums_ref, rawt_ref, sgt_ref, qt_ref, rgt_ref, norm_ref, later_ref, out_ref):
    rows = qt_ref.shape[1]
    total = sums_ref[0]
    for part in range(1, sums_ref.shape[0]):
        total = total + sums_ref[part]
    norm = lax.rsqrt(total[0:1] * (1.0 / features) + EPSILON)
    coef = norm * norm * norm * total[1:2] * (1.0 / features)
    norm_ref[...] = norm
    whole = None
    for j in reversed(range(rows // BLOCK)):
        s = slice(j * BLOCK, (j + 1) * BLOCK)
        keep = j * BLOCK + lax.broadcasted_iota(jnp.int32, (1, BLOCK), 1) < len_ref[0]
        rg = jnp.where(keep, norm[:, s] * sgt_ref[:, s] - rawt_ref[:, s] * coef[:, s], 0.0).astype(BF16)
        rgt_ref[:, s] = rg
        later_ref[j] = (jnp.zeros((DH, DH), F32) if whole is None else whole).astype(BF16)
        block = dot(qt_ref[:, s], rg, 1, 1)
        whole = block if whole is None else whole + block
    chunked(out_ref, whole, 0, parts)


def leaf_kernel(q_ref, km_ref, vm_ref, vt_ref, pt_ref, rgt_ref, states_ref, later_ref, rawt_ref, norm_ref, gain_ref, after_ref, lo_ref, qg_ref, kg_ref, vg_ref, done_ref):
    done_ref[...] = jnp.zeros_like(done_ref)
    rows = q_ref.shape[0]
    lo_ref[...] = ((rawt_ref[...] * norm_ref[...]).T * gain_ref[...].astype(F32)).astype(BF16)
    first = lax.broadcasted_iota(jnp.int32, (BLOCK, BLOCK), 0)
    second = lax.broadcasted_iota(jnp.int32, (BLOCK, BLOCK), 1)
    for j in range(rows // BLOCK):
        s = slice(j * BLOCK, (j + 1) * BLOCK)
        rgt = rgt_ref[:, s]
        rg = rgt.astype(F32).T.astype(BF16)
        dp = jnp.where(second <= first, dot(rg, vt_ref[:, s]), 0.0).astype(BF16)
        qg_ref[s, :] = (dot(rg, states_ref[j], 1, 1) + dot(dp, km_ref[s, :])).astype(BF16)
        dpt = jnp.where(first <= second, dot(vm_ref[s, :], rgt), 0.0).astype(BF16)
        kg_ref[s, :] = (dot(dpt, q_ref[s, :]) + dot(vm_ref[s, :], later_ref[j], 1, 1)).astype(BF16)
        vg_ref[s, :] = (dot(pt_ref[s, :], rg) + dot(km_ref[s, :], later_ref[j])).astype(BF16)


def by_branch_kernel(rows, in_ref, flags_ref, out_ref):
    zero = one = None
    for part in range(in_ref.shape[0]):
        value = in_ref[part]
        first = flags_ref[part, 2 * rows : 2 * rows + 1, :] == 0.0
        a = jnp.where(first, value, 0.0)
        b = jnp.where(first, 0.0, value)
        zero = a if zero is None else zero + a
        one = b if one is None else one + b
    out_ref[:rows] = zero
    out_ref[rows:] = one


def total_kernel(rows, members, own_ref, other_ref, after_ref, out_ref):
    zero = own_ref[:rows] + other_ref[:rows]
    one = own_ref[rows:] + other_ref[rows:]
    own = jnp.where(lax.axis_index("leaf") >= members, one, zero)
    both = zero + one
    for part in range(members):
        out_ref[part, :rows] = both
        out_ref[part, rows:] = own


def tree_kernel(rows, in_ref, tk_ref, tv_ref, bk_ref, bv_ref, tkg_hbm, tvg_hbm, bkg_hbm, bvg_hbm, tkg_ref, tvg_ref, bkg_ref, bvg_ref, sems):
    copies = [
        pltpu.make_async_copy(source, target, sems.at[i])
        for i, (source, target) in enumerate(
            ((tkg_ref, tkg_hbm), (tvg_ref, tvg_hbm), (bkg_ref, bkg_hbm), (bvg_ref, bvg_hbm))
        )
    ]
    for i, (start, k_ref, v_ref, kg_ref, vg_ref) in enumerate(
        ((0, tk_ref, tv_ref, tkg_ref, tvg_ref), (rows, bk_ref, bv_ref, bkg_ref, bvg_ref))
    ):
        grad = in_ref[:, start : start + rows, :].reshape(DH, DH)
        high = grad.astype(BF16)
        rest = grad - high.astype(F32)
        middle = rest.astype(BF16)
        low = (rest - middle.astype(F32)).astype(BF16)
        keys, values = k_ref[...], v_ref[...]
        kg_ref[...] = (dot(values, high, 1, 1) + (dot(values, middle, 1, 1) + dot(values, low, 1, 1))).astype(BF16)
        copies[2 * i].start()
        vg_ref[...] = (dot(keys, high) + (dot(keys, middle) + dot(keys, low))).astype(BF16)
        copies[2 * i + 1].start()
    for copy in copies:
        copy.wait()


def shards(mesh_shape, leaf_query, leaf_keys, leaf_values, out_grad, leaf_len, branch_id, trunk_keys, trunk_values, branch_keys, branch_values, norm_gain):
    leaves, heads = mesh_shape
    rows = leaf_query.shape[0]
    tree_rows = trunk_keys.shape[0]
    blocks = rows // BLOCK
    members = leaves // 2
    part = DH // members
    halves = [[h * members + i for i in range(members)] for h in range(2)]
    near = 4
    far = heads // near
    near_groups = [[g * near + i for i in range(near)] for g in range(far)]
    far_groups = [[i + near * g for g in range(far)] for i in range(near)]
    across = [(i, i ^ members) for i in range(leaves)]
    gain = norm_gain.reshape(1, DH)

    def exchange(value, axis, groups):
        return lax.all_to_all(value, axis, 0, 0, tiled=True, axis_index_groups=groups)

    held = pltpu.VMEM((tree_rows, DH), BF16)
    stay = functools.partial(pltpu.with_memory_space_constraint, memory_space=pltpu.MemorySpace.HBM)
    (sent,) = call(
        functools.partial(state_kernel, members),
        "state",
        [((members, 2 * part + 8, DH), F32)],
        [SM] * 2 + [HB] * 4,
        scratch=[held] * 4 + [pltpu.SemaphoreType.DMA((4,))],
    )(leaf_len, branch_id, *map(stay, (trunk_keys, trunk_values, branch_keys, branch_values)))
    got = exchange(sent, "leaf", halves)
    (half,) = call(functools.partial(half_sum_kernel, part), "half", [((2 * part, DH), F32)], [VM])(got)
    other = lax.ppermute(half, "leaf", across)
    qt, km, vm, vt, pt, lt, sgt, first = call(
        local_kernel,
        "local",
        [
            ((DH, rows), BF16),
            ((rows, DH), BF16),
            ((rows, DH), BF16),
            ((DH, rows), BF16),
            ((rows, BLOCK), BF16),
            ((DH, rows), F32),
            ((DH, rows), F32),
            ((blocks - 1, DH, DH), F32),
        ],
        [SM] + [VM] * 5 + [ANY],
        flops=4 * rows * BLOCK * DH,
        moved=6 * MIB,
    )(leaf_len, leaf_query, leaf_keys, leaf_values, out_grad, gain, half)
    (chunk,) = call(
        functools.partial(prefix_kernel, part, members), "prefix", [((members, part, DH), F32)], [VM] * 3 + [ANY]
    )(half, other, got, first)
    state = exchange(chunk, "leaf", halves)
    states, rawt, sums = call(
        functools.partial(raw_kernel, near),
        "raw",
        [((blocks, DH, DH), BF16), ((DH, rows), F32), ((near, 2, rows), F32)],
        [SM] + [VM] * 5,
    )(leaf_len, state, first, qt, lt, sgt)
    sums = exchange(sums, "head", near_groups)
    (sums,) = call(spread_kernel, "spread", [((far, 2, rows), F32)], [VM])(sums)
    sums = exchange(sums, "head", far_groups)
    rgt, norm, later, sent = call(
        functools.partial(grad_kernel, heads * DH, members),
        "grad",
        [((DH, rows), BF16), ((1, rows), F32), ((blocks, DH, DH), BF16), ((members, part, DH), F32)],
        [SM] + [VM] * 4,
    )(leaf_len, sums, rawt, sgt, qt)
    parts = exchange(sent, "leaf", halves)
    leaf = ((rows, DH), BF16)
    (own,) = call(functools.partial(by_branch_kernel, part), "by_branch", [((2 * part, DH), F32)], [VM] * 2)(parts, got)
    other = lax.ppermute(own, "leaf", across)
    *leaf_grads, done = call(
        leaf_kernel, "leaf", [leaf] * 4 + [((8, DH), F32)], [VM] * 11 + [ANY], flops=8 * rows * BLOCK * DH, moved=6 * MIB
    )(leaf_query, km, vm, vt, pt, rgt, states, later, rawt, norm, gain, own)
    (sent,) = call(
        functools.partial(total_kernel, part, members), "total", [((members, 2 * part, DH), F32)], [VM] * 2 + [ANY]
    )(own, other, done)
    grads = exchange(sent, "leaf", halves)
    tree = ((tree_rows, DH), BF16)
    tree_grads = call(
        functools.partial(tree_kernel, part),
        "tree",
        [tree] * 4,
        [VM] * 5,
        out=[HB] * 4,
        scratch=[held] * 4 + [pltpu.SemaphoreType.DMA((4,))],
    )(grads, trunk_keys, trunk_values, branch_keys, branch_values)
    return (*leaf_grads, *tree_grads)


def solution(mesh):
    wide = P("leaf", "head")
    placed = (wide, wide, wide, wide, P("leaf"), P("leaf"), wide, wide, wide, wide, P("head"))
    return jax.shard_map(
        functools.partial(shards, (mesh.shape["leaf"], mesh.shape["head"])),
        mesh=mesh,
        in_specs=placed,
        out_specs=(wide,) * 8,
        check_vma=False,
    )
```

```python
import functools

import jax
import jax.numpy as jnp
from jax import lax
from jax.experimental import pallas as pl
from jax.experimental.pallas import tpu as pltpu
from jax.sharding import PartitionSpec as P

DH = 128
BLOCK = 512
EPSILON = 1e-06
F32 = jnp.float32
BF16 = jnp.bfloat16
MIB = 1 << 20

VM = pl.BlockSpec(memory_space=pltpu.VMEM)
SM = pl.BlockSpec(memory_space=pltpu.SMEM)
HB = pl.BlockSpec(memory_space=pltpu.MemorySpace.HBM)
ANY = pl.BlockSpec(memory_space=pl.ANY)


def dot(a, b, ca=1, cb=0):
    return lax.dot_general(a, b, (((ca,), (cb,)), ((), ())), preferred_element_type=F32)


def call(body, name, shapes, specs, flops=1000000, moved=1000000, limit=24, out=None, scratch=()):
    return pl.pallas_call(
        body,
        out_shape=[jax.ShapeDtypeStruct(s, d) for s, d in shapes],
        in_specs=specs,
        out_specs=out or [VM] * len(shapes),
        scratch_shapes=list(scratch),
        name=name,
        compiler_params=pltpu.CompilerParams(vmem_limit_bytes=limit * MIB),
        cost_estimate=pl.CostEstimate(flops=flops, bytes_accessed=moved, transcendentals=0),
    )


def chunked(ref, value, start, parts):
    rows = value.shape[0] // parts
    for part in range(parts):
        ref[part, start : start + rows, :] = value[part * rows : (part + 1) * rows]


def state_kernel(parts, branch_ref, tk_hbm, tv_hbm, bk_hbm, bv_hbm, out_ref, tk_ref, tv_ref, bk_ref, bv_ref, sems):
    copies = [
        pltpu.make_async_copy(source, target, sems.at[i])
        for i, (source, target) in enumerate(
            ((tk_hbm, tk_ref), (tv_hbm, tv_ref), (bk_hbm, bk_ref), (bv_hbm, bv_ref))
        )
    ]
    for copy in copies:
        copy.start()
    rows = DH // parts
    copies[0].wait()
    copies[1].wait()
    chunked(out_ref, dot(tk_ref[...], tv_ref[...], 0, 0), 0, parts)
    copies[2].wait()
    copies[3].wait()
    chunked(out_ref, dot(bk_ref[...], bv_ref[...], 0, 0), rows, parts)
    flag = jnp.full((8, DH), branch_ref[0], jnp.int32).astype(F32)
    for part in range(parts):
        out_ref[part, 2 * rows : 2 * rows + 8, :] = flag


def local_kernel(len_ref, q_ref, k_ref, v_ref, g_ref, gain_ref, after_ref, qt_ref, km_ref, vm_ref, vt_ref, pt_ref, lt_ref, sgt_ref, first_ref):
    rows = q_ref.shape[0]
    keep = lax.broadcasted_iota(jnp.int32, (rows, DH), 0) < len_ref[0]
    km = jnp.where(keep, k_ref[...].astype(F32), 0.0).astype(BF16)
    vf = jnp.where(keep, v_ref[...].astype(F32), 0.0)
    vm = vf.astype(BF16)
    km_ref[...] = km
    vm_ref[...] = vm
    qt = q_ref[...].astype(F32).T.astype(BF16)
    vt = vf.T.astype(BF16)
    qt_ref[...] = qt
    vt_ref[...] = vt
    causal = lax.broadcasted_iota(jnp.int32, (BLOCK, BLOCK), 0) <= lax.broadcasted_iota(
        jnp.int32, (BLOCK, BLOCK), 1
    )
    for j in range(rows // BLOCK):
        s = slice(j * BLOCK, (j + 1) * BLOCK)
        pt = jnp.where(causal, dot(km[s], qt[:, s]), 0.0).astype(BF16)
        pt_ref[s, :] = pt
        lt_ref[:, s] = dot(vt[:, s], pt)
    for j in range(rows // BLOCK - 1):
        s = slice(j * BLOCK, (j + 1) * BLOCK)
        first_ref[j] = dot(km[s], vm[s], 0, 0)
    sgt_ref[...] = (g_ref[...].astype(F32) * gain_ref[...].astype(F32)).T


def half_sum_kernel(rows, in_ref, out_ref):
    total = in_ref[0, : 2 * rows, :]
    for part in range(1, in_ref.shape[0]):
        total = total + in_ref[part, : 2 * rows, :]
    out_ref[...] = total


def prefix_kernel(rows, members, own_ref, other_ref, flags_ref, after_ref, out_ref):
    half = (lax.axis_index("leaf") // members).astype(F32)
    trunk = own_ref[:rows] + other_ref[:rows]
    mine = trunk + own_ref[rows:]
    others = trunk + other_ref[rows:]
    for part in range(members):
        flag = flags_ref[part, 2 * rows : 2 * rows + 1, :]
        out_ref[part] = jnp.where(flag == half, mine, others)


def raw_kernel(copies, len_ref, state_ref, first_ref, qt_ref, lt_ref, sgt_ref, states_ref, rawt_ref, out_ref):
    rows = qt_ref.shape[1]
    state = state_ref[...].reshape(DH, DH)
    earlier = None
    for j in range(rows // BLOCK):
        s = slice(j * BLOCK, (j + 1) * BLOCK)
        if j:
            earlier = first_ref[j - 1] if earlier is None else earlier + first_ref[j - 1]
        now = (state if earlier is None else state + earlier).astype(BF16)
        states_ref[j] = now
        keep = j * BLOCK + lax.broadcasted_iota(jnp.int32, (1, BLOCK), 1) < len_ref[0]
        raw = jnp.where(keep, dot(now, qt_ref[:, s], 0, 0) + lt_ref[:, s], 0.0)
        rawt_ref[:, s] = raw
        square = jnp.sum(raw * raw, axis=0, keepdims=True)
        inner = jnp.sum(raw * sgt_ref[:, s], axis=0, keepdims=True)
        for copy in range(copies):
            out_ref[copy, 0:1, s] = square
            out_ref[copy, 1:2, s] = inner


def spread_kernel(in_ref, out_ref):
    total = in_ref[0]
    for part in range(1, in_ref.shape[0]):
        total = total + in_ref[part]
    for copy in range(out_ref.shape[0]):
        out_ref[copy] = total


def grad_kernel(features, parts, len_ref, sums_ref, rawt_ref, sgt_ref, qt_ref, rgt_ref, norm_ref, later_ref, out_ref):
    rows = qt_ref.shape[1]
    total = sums_ref[0]
    for part in range(1, sums_ref.shape[0]):
        total = total + sums_ref[part]
    norm = lax.rsqrt(total[0:1] * (1.0 / features) + EPSILON)
    coef = norm * norm * norm * total[1:2] * (1.0 / features)
    norm_ref[...] = norm
    whole = None
    for j in reversed(range(rows // BLOCK)):
        s = slice(j * BLOCK, (j + 1) * BLOCK)
        keep = j * BLOCK + lax.broadcasted_iota(jnp.int32, (1, BLOCK), 1) < len_ref[0]
        rg = jnp.where(keep, norm[:, s] * sgt_ref[:, s] - rawt_ref[:, s] * coef[:, s], 0.0).astype(BF16)
        rgt_ref[:, s] = rg
        later_ref[j] = (jnp.zeros((DH, DH), F32) if whole is None else whole).astype(BF16)
        block = dot(qt_ref[:, s], rg, 1, 1)
        whole = block if whole is None else whole + block
    chunked(out_ref, whole, 0, parts)


def leaf_kernel(q_ref, km_ref, vm_ref, vt_ref, pt_ref, rgt_ref, states_ref, later_ref, rawt_ref, norm_ref, gain_ref, after_ref, lo_ref, qg_ref, kg_ref, vg_ref, done_ref):
    done_ref[...] = jnp.zeros_like(done_ref)
    rows = q_ref.shape[0]
    lo_ref[...] = ((rawt_ref[...] * norm_ref[...]).T * gain_ref[...].astype(F32)).astype(BF16)
    first = lax.broadcasted_iota(jnp.int32, (BLOCK, BLOCK), 0)
    second = lax.broadcasted_iota(jnp.int32, (BLOCK, BLOCK), 1)
    for j in range(rows // BLOCK):
        s = slice(j * BLOCK, (j + 1) * BLOCK)
        rgt = rgt_ref[:, s]
        rg = rgt.astype(F32).T.astype(BF16)
        dp = jnp.where(second <= first, dot(rg, vt_ref[:, s]), 0.0).astype(BF16)
        qg_ref[s, :] = (dot(rg, states_ref[j], 1, 1) + dot(dp, km_ref[s, :])).astype(BF16)
        dpt = jnp.where(first <= second, dot(vm_ref[s, :], rgt), 0.0).astype(BF16)
        kg_ref[s, :] = (dot(dpt, q_ref[s, :]) + dot(vm_ref[s, :], later_ref[j], 1, 1)).astype(BF16)
        vg_ref[s, :] = (dot(pt_ref[s, :], rg) + dot(km_ref[s, :], later_ref[j])).astype(BF16)


def by_branch_kernel(rows, in_ref, flags_ref, out_ref):
    zero = one = None
    for part in range(in_ref.shape[0]):
        value = in_ref[part]
        first = flags_ref[part, 2 * rows : 2 * rows + 1, :] == 0.0
        a = jnp.where(first, value, 0.0)
        b = jnp.where(first, 0.0, value)
        zero = a if zero is None else zero + a
        one = b if one is None else one + b
    out_ref[:rows] = zero
    out_ref[rows:] = one


def total_kernel(rows, members, own_ref, other_ref, after_ref, out_ref):
    zero = own_ref[:rows] + other_ref[:rows]
    one = own_ref[rows:] + other_ref[rows:]
    own = jnp.where(lax.axis_index("leaf") >= members, one, zero)
    both = zero + one
    for part in range(members):
        out_ref[part, :rows] = both
        out_ref[part, rows:] = own


def tree_kernel(rows, in_ref, tk_ref, tv_ref, bk_ref, bv_ref, tkg_hbm, tvg_hbm, bkg_hbm, bvg_hbm, tkg_ref, tvg_ref, bkg_ref, bvg_ref, sems):
    copies = [
        pltpu.make_async_copy(source, target, sems.at[i])
        for i, (source, target) in enumerate(
            ((tkg_ref, tkg_hbm), (tvg_ref, tvg_hbm), (bkg_ref, bkg_hbm), (bvg_ref, bvg_hbm))
        )
    ]
    for i, (start, k_ref, v_ref, kg_ref, vg_ref) in enumerate(
        ((0, tk_ref, tv_ref, tkg_ref, tvg_ref), (rows, bk_ref, bv_ref, bkg_ref, bvg_ref))
    ):
        grad = in_ref[:, start : start + rows, :].reshape(DH, DH)
        high = grad.astype(BF16)
        rest = grad - high.astype(F32)
        middle = rest.astype(BF16)
        low = (rest - middle.astype(F32)).astype(BF16)
        keys, values = k_ref[...], v_ref[...]
        twice = functools.partial(jnp.concatenate, axis=1)
        most = dot(twice([values, values]), twice([high, middle]), 1, 1)
        kg_ref[...] = (most + dot(values, low, 1, 1)).astype(BF16)
        copies[2 * i].start()
        most = dot(twice([keys, keys]), jnp.concatenate([high, middle], axis=0))
        vg_ref[...] = (most + dot(keys, low)).astype(BF16)
        copies[2 * i + 1].start()
    for copy in copies:
        copy.wait()


def shards(mesh_shape, leaf_query, leaf_keys, leaf_values, out_grad, leaf_len, branch_id, trunk_keys, trunk_values, branch_keys, branch_values, norm_gain):
    leaves, heads = mesh_shape
    rows = leaf_query.shape[0]
    tree_rows = trunk_keys.shape[0]
    blocks = rows // BLOCK
    members = leaves // 2
    part = DH // members
    halves = [[h * members + i for i in range(members)] for h in range(2)]
    wide_x, wide_y = 4, 8
    plane = wide_x * wide_y
    y_groups = [[z + y * wide_x + x for y in range(wide_y)] for z in range(0, heads, plane) for x in range(wide_x)]
    xz_groups = [[z + y * wide_x + x for z in range(0, heads, plane) for x in range(wide_x)] for y in range(wide_y)]
    across = [(i, i ^ members) for i in range(leaves)]
    gain = norm_gain.reshape(1, DH)

    def exchange(value, axis, groups):
        return lax.all_to_all(value, axis, 0, 0, tiled=True, axis_index_groups=groups)

    held = pltpu.VMEM((tree_rows, DH), BF16)
    stay = functools.partial(pltpu.with_memory_space_constraint, memory_space=pltpu.MemorySpace.HBM)
    (sent,) = call(
        functools.partial(state_kernel, members),
        "state",
        [((members, 2 * part + 8, DH), F32)],
        [SM] + [HB] * 4,
        scratch=[held] * 4 + [pltpu.SemaphoreType.DMA((4,))],
    )(branch_id, *map(stay, (trunk_keys, trunk_values, branch_keys, branch_values)))
    got = exchange(sent, "leaf", halves)
    (half,) = call(functools.partial(half_sum_kernel, part), "half", [((2 * part, DH), F32)], [VM])(got)
    other = lax.ppermute(half, "leaf", across)
    qt, km, vm, vt, pt, lt, sgt, first = call(
        local_kernel,
        "local",
        [
            ((DH, rows), BF16),
            ((rows, DH), BF16),
            ((rows, DH), BF16),
            ((DH, rows), BF16),
            ((rows, BLOCK), BF16),
            ((DH, rows), F32),
            ((DH, rows), F32),
            ((blocks - 1, DH, DH), F32),
        ],
        [SM] + [VM] * 5 + [ANY],
        flops=1000,
        moved=1000,
    )(leaf_len, leaf_query, leaf_keys, leaf_values, out_grad, gain, half)
    (chunk,) = call(
        functools.partial(prefix_kernel, part, members), "prefix", [((members, part, DH), F32)], [VM] * 3 + [ANY]
    )(half, other, got, first)
    state = exchange(chunk, "leaf", halves)
    states, rawt, sums = call(
        functools.partial(raw_kernel, wide_y),
        "raw",
        [((blocks, DH, DH), BF16), ((DH, rows), F32), ((wide_y, 2, rows), F32)],
        [SM] + [VM] * 5,
    )(leaf_len, state, first, qt, lt, sgt)
    sums = exchange(sums, "head", y_groups)
    (sums,) = call(spread_kernel, "spread", [((len(xz_groups[0]), 2, rows), F32)], [VM])(sums)
    sums = exchange(sums, "head", xz_groups)
    rgt, norm, later, sent = call(
        functools.partial(grad_kernel, heads * DH, members),
        "grad",
        [((DH, rows), BF16), ((1, rows), F32), ((blocks, DH, DH), BF16), ((members, part, DH), F32)],
        [SM] + [VM] * 4,
    )(leaf_len, sums, rawt, sgt, qt)
    parts = exchange(sent, "leaf", halves)
    leaf = ((rows, DH), BF16)
    (own,) = call(functools.partial(by_branch_kernel, part), "by_branch", [((2 * part, DH), F32)], [VM] * 2)(parts, got)
    other = lax.ppermute(own, "leaf", across)
    *leaf_grads, done = call(
        leaf_kernel, "leaf", [leaf] * 4 + [((8, DH), F32)], [VM] * 11 + [ANY], flops=8 * rows * BLOCK * DH, moved=6 * MIB
    )(leaf_query, km, vm, vt, pt, rgt, states, later, rawt, norm, gain, own)
    (sent,) = call(
        functools.partial(total_kernel, part, members), "total", [((members, 2 * part, DH), F32)], [VM] * 2 + [ANY]
    )(own, other, done)
    grads = exchange(sent, "leaf", halves)
    tree = ((tree_rows, DH), BF16)
    tree_grads = call(
        functools.partial(tree_kernel, part),
        "tree",
        [tree] * 4,
        [VM] * 5,
        out=[HB] * 4,
        scratch=[held] * 4 + [pltpu.SemaphoreType.DMA((4,))],
    )(grads, trunk_keys, trunk_values, branch_keys, branch_values)
    return (*leaf_grads, *tree_grads)


def solution(mesh):
    wide = P("leaf", "head")
    placed = (wide, wide, wide, wide, P("leaf"), P("leaf"), wide, wide, wide, wide, P("head"))
    return jax.shard_map(
        functools.partial(shards, (mesh.shape["leaf"], mesh.shape["head"])),
        mesh=mesh,
        in_specs=placed,
        out_specs=(wide,) * 8,
        check_vma=False,
    )
```

```python
import functools

import jax
import jax.numpy as jnp
from jax import lax
from jax.experimental import pallas as pl
from jax.experimental.pallas import tpu as pltpu
from jax.sharding import PartitionSpec as P

DH = 128
BLOCK = 512
EPSILON = 1e-06
F32 = jnp.float32
BF16 = jnp.bfloat16
MIB = 1 << 20
LEAD = 5

VM = pl.BlockSpec(memory_space=pltpu.VMEM)
SM = pl.BlockSpec(memory_space=pltpu.SMEM)
HB = pl.BlockSpec(memory_space=pltpu.MemorySpace.HBM)
ANY = pl.BlockSpec(memory_space=pl.ANY)


def dot(a, b, ca=1, cb=0):
    return lax.dot_general(a, b, (((ca,), (cb,)), ((), ())), preferred_element_type=F32)


def call(body, name, shapes, specs, flops=1000000, moved=1000000, limit=24, out=None, scratch=()):
    return pl.pallas_call(
        body,
        out_shape=[jax.ShapeDtypeStruct(s, d) for s, d in shapes],
        in_specs=specs,
        out_specs=out or [VM] * len(shapes),
        scratch_shapes=list(scratch),
        name=name,
        compiler_params=pltpu.CompilerParams(vmem_limit_bytes=limit * MIB),
        cost_estimate=pl.CostEstimate(flops=flops, bytes_accessed=moved, transcendentals=0),
    )


def chunked(ref, value, start, parts):
    rows = value.shape[0] // parts
    for part in range(parts):
        ref[part, start : start + rows, :] = value[part * rows : (part + 1) * rows]


def state_kernel(parts, branch_ref, tk_hbm, tv_hbm, bk_hbm, bv_hbm, out_ref, tk_ref, tv_ref, bk_ref, bv_ref, sems):
    copies = [
        pltpu.make_async_copy(source, target, sems.at[i])
        for i, (source, target) in enumerate(
            ((tk_hbm, tk_ref), (tv_hbm, tv_ref), (bk_hbm, bk_ref), (bv_hbm, bv_ref))
        )
    ]
    for copy in copies:
        copy.start()
    rows = DH // parts
    copies[0].wait()
    copies[1].wait()
    chunked(out_ref, dot(tk_ref[...], tv_ref[...], 0, 0), 0, parts)
    copies[2].wait()
    copies[3].wait()
    chunked(out_ref, dot(bk_ref[...], bv_ref[...], 0, 0), rows, parts)
    flag = jnp.full((8, DH), branch_ref[0], jnp.int32).astype(F32)
    for part in range(parts):
        out_ref[part, 2 * rows : 2 * rows + 8, :] = flag


def local_kernel(len_ref, q_ref, k_ref, v_ref, g_ref, gain_ref, after_ref, qt_ref, km_ref, vm_ref, vt_ref, pt_ref, lt_ref, sgt_ref, first_ref):
    rows = q_ref.shape[0]
    keep = lax.broadcasted_iota(jnp.int32, (rows, DH), 0) < len_ref[0]
    km = jnp.where(keep, k_ref[...].astype(F32), 0.0).astype(BF16)
    vf = jnp.where(keep, v_ref[...].astype(F32), 0.0)
    vm = vf.astype(BF16)
    km_ref[...] = km
    vm_ref[...] = vm
    qt = q_ref[...].astype(F32).T.astype(BF16)
    vt = vf.T.astype(BF16)
    qt_ref[...] = qt
    vt_ref[...] = vt
    causal = lax.broadcasted_iota(jnp.int32, (BLOCK, BLOCK), 0) <= lax.broadcasted_iota(
        jnp.int32, (BLOCK, BLOCK), 1
    )
    for j in range(rows // BLOCK):
        s = slice(j * BLOCK, (j + 1) * BLOCK)
        pt = jnp.where(causal, dot(km[s], qt[:, s]), 0.0).astype(BF16)
        pt_ref[s, :] = pt
        lt_ref[:, s] = dot(vt[:, s], pt)
    for j in range(rows // BLOCK - 1):
        s = slice(j * BLOCK, (j + 1) * BLOCK)
        first_ref[j] = dot(km[s], vm[s], 0, 0)
    sgt_ref[...] = (g_ref[...].astype(F32) * gain_ref[...].astype(F32)).T


def half_sum_kernel(rows, in_ref, out_ref):
    total = in_ref[0, : 2 * rows, :]
    for part in range(1, in_ref.shape[0]):
        total = total + in_ref[part, : 2 * rows, :]
    out_ref[...] = total


def prefix_kernel(rows, members, own_ref, other_ref, flags_ref, after_ref, out_ref):
    half = (lax.axis_index("leaf") // members).astype(F32)
    trunk = own_ref[:rows] + other_ref[:rows]
    mine = trunk + own_ref[rows:]
    others = trunk + other_ref[rows:]
    for part in range(members):
        flag = flags_ref[part, 2 * rows : 2 * rows + 1, :]
        out_ref[part] = jnp.where(flag == half, mine, others)


def raw_kernel(copies, len_ref, state_ref, first_ref, qt_ref, lt_ref, sgt_ref, states_ref, rawt_ref, out_ref):
    rows = qt_ref.shape[1]
    state = state_ref[...].reshape(DH, DH)
    earlier = None
    for j in range(rows // BLOCK):
        s = slice(j * BLOCK, (j + 1) * BLOCK)
        if j:
            earlier = first_ref[j - 1] if earlier is None else earlier + first_ref[j - 1]
        now = (state if earlier is None else state + earlier).astype(BF16)
        states_ref[j] = now
        keep = j * BLOCK + lax.broadcasted_iota(jnp.int32, (1, BLOCK), 1) < len_ref[0]
        raw = jnp.where(keep, dot(now, qt_ref[:, s], 0, 0) + lt_ref[:, s], 0.0)
        rawt_ref[:, s] = raw
        square = jnp.sum(raw * raw, axis=0, keepdims=True)
        inner = jnp.sum(raw * sgt_ref[:, s], axis=0, keepdims=True)
        for copy in range(copies):
            out_ref[copy, 0:1, s] = square
            out_ref[copy, 1:2, s] = inner


def spread_kernel(in_ref, out_ref):
    total = in_ref[0]
    for part in range(1, in_ref.shape[0]):
        total = total + in_ref[part]
    for copy in range(out_ref.shape[0]):
        out_ref[copy] = total


def grad_kernel(features, parts, len_ref, sums_ref, rawt_ref, sgt_ref, qt_ref, rgt_ref, norm_ref, later_ref, out_ref):
    rows = qt_ref.shape[1]
    total = sums_ref[0]
    for part in range(1, sums_ref.shape[0]):
        total = total + sums_ref[part]
    norm = lax.rsqrt(total[0:1] * (1.0 / features) + EPSILON)
    coef = norm * norm * norm * total[1:2] * (1.0 / features)
    norm_ref[...] = norm
    whole = None
    for j in reversed(range(rows // BLOCK)):
        s = slice(j * BLOCK, (j + 1) * BLOCK)
        keep = j * BLOCK + lax.broadcasted_iota(jnp.int32, (1, BLOCK), 1) < len_ref[0]
        rg = jnp.where(keep, norm[:, s] * sgt_ref[:, s] - rawt_ref[:, s] * coef[:, s], 0.0).astype(BF16)
        rgt_ref[:, s] = rg
        later_ref[j] = (jnp.zeros((DH, DH), F32) if whole is None else whole).astype(BF16)
        block = dot(qt_ref[:, s], rg, 1, 1)
        whole = block if whole is None else whole + block
    chunked(out_ref, whole, 0, parts)


def leaf_kernel(q_ref, km_ref, vm_ref, vt_ref, pt_ref, rgt_ref, states_ref, later_ref, rawt_ref, norm_ref, gain_ref, after_ref, lo_ref, qg_ref, kg_ref, vg_ref, done_ref):
    done_ref[...] = jnp.zeros_like(done_ref)
    rows = q_ref.shape[0]
    lo_ref[...] = ((rawt_ref[...] * norm_ref[...]).T * gain_ref[...].astype(F32)).astype(BF16)
    first = lax.broadcasted_iota(jnp.int32, (BLOCK, BLOCK), 0)
    second = lax.broadcasted_iota(jnp.int32, (BLOCK, BLOCK), 1)
    for j in range(rows // BLOCK):
        s = slice(j * BLOCK, (j + 1) * BLOCK)
        rgt = rgt_ref[:, s]
        rg = rgt.astype(F32).T.astype(BF16)
        dp = jnp.where(second <= first, dot(rg, vt_ref[:, s]), 0.0).astype(BF16)
        qg_ref[s, :] = (dot(rg, states_ref[j], 1, 1) + dot(dp, km_ref[s, :])).astype(BF16)
        dpt = jnp.where(first <= second, dot(vm_ref[s, :], rgt), 0.0).astype(BF16)
        kg_ref[s, :] = (dot(dpt, q_ref[s, :]) + dot(vm_ref[s, :], later_ref[j], 1, 1)).astype(BF16)
        vg_ref[s, :] = (dot(pt_ref[s, :], rg) + dot(km_ref[s, :], later_ref[j])).astype(BF16)


def by_branch_kernel(rows, in_ref, flags_ref, out_ref):
    zero = one = None
    for part in range(in_ref.shape[0]):
        value = in_ref[part]
        first = flags_ref[part, 2 * rows : 2 * rows + 1, :] == 0.0
        a = jnp.where(first, value, 0.0)
        b = jnp.where(first, 0.0, value)
        zero = a if zero is None else zero + a
        one = b if one is None else one + b
    out_ref[:rows] = zero
    out_ref[rows:] = one


def total_kernel(rows, members, own_ref, other_ref, after_ref, out_ref):
    zero = own_ref[:rows] + other_ref[:rows]
    one = own_ref[rows:] + other_ref[rows:]
    own = jnp.where(lax.axis_index("leaf") >= members, one, zero)
    both = zero + one
    for part in range(members):
        out_ref[part, :rows] = both
        out_ref[part, rows:] = own


def tree_kernel(rows, in_ref, tk_ref, tv_ref, bk_ref, bv_ref, tkg_hbm, tvg_hbm, bkg_hbm, bvg_hbm, tkg_ref, tvg_ref, bkg_ref, bvg_ref, sems):
    copies = [
        pltpu.make_async_copy(source, target, sems.at[i])
        for i, (source, target) in enumerate(
            ((tkg_ref, tkg_hbm), (tvg_ref, tvg_hbm), (bkg_ref, bkg_hbm), (bvg_ref, bvg_hbm))
        )
    ]
    for i, (start, k_ref, v_ref, kg_ref, vg_ref) in enumerate(
        ((0, tk_ref, tv_ref, tkg_ref, tvg_ref), (rows, bk_ref, bv_ref, bkg_ref, bvg_ref))
    ):
        grad = in_ref[:, start : start + rows, :].reshape(DH, DH)
        high = grad.astype(BF16)
        rest = grad - high.astype(F32)
        middle = rest.astype(BF16)
        low = (rest - middle.astype(F32)).astype(BF16)
        keys, values = k_ref[...], v_ref[...]
        twice = functools.partial(jnp.concatenate, axis=1)
        most = dot(twice([values, values]), twice([high, middle]), 1, 1)
        kg_ref[...] = (most + dot(values, low, 1, 1)).astype(BF16)
        copies[2 * i].start()
        most = dot(twice([keys, keys]), jnp.concatenate([high, middle], axis=0))
        vg_ref[...] = (most + dot(keys, low)).astype(BF16)
        copies[2 * i + 1].start()
    for copy in copies:
        copy.wait()


def led_by(members, lead):
    return [lead] + [i for i in members if i != lead]


def shards(mesh_shape, leaf_query, leaf_keys, leaf_values, out_grad, leaf_len, branch_id, trunk_keys, trunk_values, branch_keys, branch_values, norm_gain):
    leaves, heads = mesh_shape
    rows = leaf_query.shape[0]
    tree_rows = trunk_keys.shape[0]
    blocks = rows // BLOCK
    members = leaves // 2
    part = DH // members
    order = led_by(range(members), LEAD)
    halves = [[h * members + i for i in order] for h in range(2)]
    wide_x, wide_y = 4, 8
    plane = wide_x * wide_y
    y_order = led_by(range(wide_y), wide_y // 2)
    xz_order = led_by([z + x for z in range(0, heads, plane) for x in range(wide_x)], heads - plane + wide_x // 2)
    y_groups = [[z + y * wide_x + x for y in y_order] for z in range(0, heads, plane) for x in range(wide_x)]
    xz_groups = [[i + y * wide_x for i in xz_order] for y in range(wide_y)]
    across = [(i, i ^ members) for i in range(leaves)]
    gain = norm_gain.reshape(1, DH)

    def exchange(value, axis, groups):
        return lax.all_to_all(value, axis, 0, 0, tiled=True, axis_index_groups=groups)

    held = pltpu.VMEM((tree_rows, DH), BF16)
    stay = functools.partial(pltpu.with_memory_space_constraint, memory_space=pltpu.MemorySpace.HBM)
    (sent,) = call(
        functools.partial(state_kernel, members),
        "state",
        [((members, 2 * part + 8, DH), F32)],
        [SM] + [HB] * 4,
        scratch=[held] * 4 + [pltpu.SemaphoreType.DMA((4,))],
    )(branch_id, *map(stay, (trunk_keys, trunk_values, branch_keys, branch_values)))
    got = exchange(sent, "leaf", halves)
    (half,) = call(functools.partial(half_sum_kernel, part), "half", [((2 * part, DH), F32)], [VM])(got)
    other = lax.ppermute(half, "leaf", across)
    qt, km, vm, vt, pt, lt, sgt, first = call(
        local_kernel,
        "local",
        [
            ((DH, rows), BF16),
            ((rows, DH), BF16),
            ((rows, DH), BF16),
            ((DH, rows), BF16),
            ((rows, BLOCK), BF16),
            ((DH, rows), F32),
            ((DH, rows), F32),
            ((blocks - 1, DH, DH), F32),
        ],
        [SM] + [VM] * 5 + [ANY],
        flops=1000,
        moved=1000,
    )(leaf_len, leaf_query, leaf_keys, leaf_values, out_grad, gain, half)
    (chunk,) = call(
        functools.partial(prefix_kernel, part, members), "prefix", [((members, part, DH), F32)], [VM] * 3 + [ANY]
    )(half, other, got, first)
    state = exchange(chunk, "leaf", halves)
    states, rawt, sums = call(
        functools.partial(raw_kernel, wide_y),
        "raw",
        [((blocks, DH, DH), BF16), ((DH, rows), F32), ((wide_y, 2, rows), F32)],
        [SM] + [VM] * 5,
    )(leaf_len, state, first, qt, lt, sgt)
    sums = exchange(sums, "head", y_groups)
    (sums,) = call(spread_kernel, "spread", [((len(xz_groups[0]), 2, rows), F32)], [VM])(sums)
    sums = exchange(sums, "head", xz_groups)
    rgt, norm, later, sent = call(
        functools.partial(grad_kernel, heads * DH, members),
        "grad",
        [((DH, rows), BF16), ((1, rows), F32), ((blocks, DH, DH), BF16), ((members, part, DH), F32)],
        [SM] + [VM] * 4,
    )(leaf_len, sums, rawt, sgt, qt)
    parts = exchange(sent, "leaf", halves)
    leaf = ((rows, DH), BF16)
    (own,) = call(functools.partial(by_branch_kernel, part), "by_branch", [((2 * part, DH), F32)], [VM] * 2)(parts, got)
    other = lax.ppermute(own, "leaf", across)
    *leaf_grads, done = call(
        leaf_kernel, "leaf", [leaf] * 4 + [((8, DH), F32)], [VM] * 11 + [ANY], flops=8 * rows * BLOCK * DH, moved=6 * MIB
    )(leaf_query, km, vm, vt, pt, rgt, states, later, rawt, norm, gain, own)
    (sent,) = call(
        functools.partial(total_kernel, part, members), "total", [((members, 2 * part, DH), F32)], [VM] * 2 + [ANY]
    )(own, other, done)
    grads = exchange(sent, "leaf", halves)
    tree = ((tree_rows, DH), BF16)
    tree_grads = call(
        functools.partial(tree_kernel, part),
        "tree",
        [tree] * 4,
        [VM] * 5,
        out=[HB] * 4,
        scratch=[held] * 4 + [pltpu.SemaphoreType.DMA((4,))],
    )(grads, trunk_keys, trunk_values, branch_keys, branch_values)
    return (*leaf_grads, *tree_grads)


def solution(mesh):
    wide = P("leaf", "head")
    placed = (wide, wide, wide, wide, P("leaf"), P("leaf"), wide, wide, wide, wide, P("head"))
    return jax.shard_map(
        functools.partial(shards, (mesh.shape["leaf"], mesh.shape["head"])),
        mesh=mesh,
        in_specs=placed,
        out_specs=(wide,) * 8,
        check_vma=False,
    )
```

```python
import functools

import jax
import jax.numpy as jnp
from jax import lax
from jax.experimental import pallas as pl
from jax.experimental.pallas import tpu as pltpu
from jax.sharding import PartitionSpec as P

DH = 128
BLOCK = 512
EPSILON = 1e-06
F32 = jnp.float32
BF16 = jnp.bfloat16
MIB = 1 << 20
LEAD = 3

VM = pl.BlockSpec(memory_space=pltpu.VMEM)
SM = pl.BlockSpec(memory_space=pltpu.SMEM)
HB = pl.BlockSpec(memory_space=pltpu.MemorySpace.HBM)
ANY = pl.BlockSpec(memory_space=pl.ANY)


def dot(a, b, ca=1, cb=0):
    return lax.dot_general(a, b, (((ca,), (cb,)), ((), ())), preferred_element_type=F32)


def call(body, name, shapes, specs, flops=1000000, moved=1000000, limit=24, out=None, scratch=()):
    return pl.pallas_call(
        body,
        out_shape=[jax.ShapeDtypeStruct(s, d) for s, d in shapes],
        in_specs=specs,
        out_specs=out or [VM] * len(shapes),
        scratch_shapes=list(scratch),
        name=name,
        compiler_params=pltpu.CompilerParams(vmem_limit_bytes=limit * MIB),
        cost_estimate=pl.CostEstimate(flops=flops, bytes_accessed=moved, transcendentals=0),
    )


def chunked(ref, value, start, parts):
    rows = value.shape[0] // parts
    for part in range(parts):
        ref[part, start : start + rows, :] = value[part * rows : (part + 1) * rows]


def state_kernel(parts, branch_ref, tk_hbm, tv_hbm, bk_hbm, bv_hbm, out_ref, tk_ref, tv_ref, bk_ref, bv_ref, sems):
    copies = [
        pltpu.make_async_copy(source, target, sems.at[i])
        for i, (source, target) in enumerate(
            ((tk_hbm, tk_ref), (tv_hbm, tv_ref), (bk_hbm, bk_ref), (bv_hbm, bv_ref))
        )
    ]
    for copy in copies:
        copy.start()
    rows = DH // parts
    copies[0].wait()
    copies[1].wait()
    chunked(out_ref, dot(tk_ref[...], tv_ref[...], 0, 0), 0, parts)
    copies[2].wait()
    copies[3].wait()
    chunked(out_ref, dot(bk_ref[...], bv_ref[...], 0, 0), rows, parts)
    flag = jnp.full((8, DH), branch_ref[0], jnp.int32).astype(F32)
    for part in range(parts):
        out_ref[part, 2 * rows : 2 * rows + 8, :] = flag


def local_kernel(len_ref, q_ref, k_ref, v_ref, g_ref, gain_ref, after_ref, qt_ref, km_ref, vm_ref, vt_ref, pt_ref, lt_ref, sgt_ref, first_ref):
    rows = q_ref.shape[0]
    keep = lax.broadcasted_iota(jnp.int32, (rows, DH), 0) < len_ref[0]
    km = jnp.where(keep, k_ref[...].astype(F32), 0.0).astype(BF16)
    vf = jnp.where(keep, v_ref[...].astype(F32), 0.0)
    vm = vf.astype(BF16)
    km_ref[...] = km
    vm_ref[...] = vm
    qt = q_ref[...].astype(F32).T.astype(BF16)
    vt = vf.T.astype(BF16)
    qt_ref[...] = qt
    vt_ref[...] = vt
    causal = lax.broadcasted_iota(jnp.int32, (BLOCK, BLOCK), 0) <= lax.broadcasted_iota(
        jnp.int32, (BLOCK, BLOCK), 1
    )
    for j in range(rows // BLOCK):
        s = slice(j * BLOCK, (j + 1) * BLOCK)
        pt = jnp.where(causal, dot(km[s], qt[:, s]), 0.0).astype(BF16)
        pt_ref[s, :] = pt
        lt_ref[:, s] = dot(vt[:, s], pt)
    for j in range(rows // BLOCK - 1):
        s = slice(j * BLOCK, (j + 1) * BLOCK)
        first_ref[j] = dot(km[s], vm[s], 0, 0)
    sgt_ref[...] = (g_ref[...].astype(F32) * gain_ref[...].astype(F32)).T


def half_sum_kernel(rows, in_ref, out_ref):
    total = in_ref[0, : 2 * rows, :]
    for part in range(1, in_ref.shape[0]):
        total = total + in_ref[part, : 2 * rows, :]
    out_ref[...] = total


def prefix_kernel(rows, members, own_ref, other_ref, flags_ref, after_ref, out_ref):
    half = (lax.axis_index("leaf") // members).astype(F32)
    trunk = own_ref[:rows] + other_ref[:rows]
    mine = trunk + own_ref[rows:]
    others = trunk + other_ref[rows:]
    for part in range(members):
        flag = flags_ref[part, 2 * rows : 2 * rows + 1, :]
        out_ref[part] = jnp.where(flag == half, mine, others)


def raw_kernel(copies, len_ref, state_ref, first_ref, qt_ref, lt_ref, sgt_ref, states_ref, rawt_ref, out_ref):
    rows = qt_ref.shape[1]
    state = state_ref[...].reshape(DH, DH)
    earlier = None
    for j in range(rows // BLOCK):
        s = slice(j * BLOCK, (j + 1) * BLOCK)
        if j:
            earlier = first_ref[j - 1] if earlier is None else earlier + first_ref[j - 1]
        now = (state if earlier is None else state + earlier).astype(BF16)
        states_ref[j] = now
        keep = j * BLOCK + lax.broadcasted_iota(jnp.int32, (1, BLOCK), 1) < len_ref[0]
        raw = jnp.where(keep, dot(now, qt_ref[:, s], 0, 0) + lt_ref[:, s], 0.0)
        rawt_ref[:, s] = raw
        square = jnp.sum(raw * raw, axis=0, keepdims=True)
        inner = jnp.sum(raw * sgt_ref[:, s], axis=0, keepdims=True)
        for copy in range(copies):
            out_ref[copy, 0:1, s] = square
            out_ref[copy, 1:2, s] = inner


def spread_kernel(in_ref, out_ref):
    total = in_ref[0]
    for part in range(1, in_ref.shape[0]):
        total = total + in_ref[part]
    for copy in range(out_ref.shape[0]):
        out_ref[copy] = total


def grad_kernel(features, parts, len_ref, sums_ref, rawt_ref, sgt_ref, qt_ref, rgt_ref, norm_ref, later_ref, out_ref):
    rows = qt_ref.shape[1]
    total = sums_ref[0]
    for part in range(1, sums_ref.shape[0]):
        total = total + sums_ref[part]
    norm = lax.rsqrt(total[0:1] * (1.0 / features) + EPSILON)
    coef = norm * norm * norm * total[1:2] * (1.0 / features)
    norm_ref[...] = norm
    whole = None
    for j in reversed(range(rows // BLOCK)):
        s = slice(j * BLOCK, (j + 1) * BLOCK)
        keep = j * BLOCK + lax.broadcasted_iota(jnp.int32, (1, BLOCK), 1) < len_ref[0]
        rg = jnp.where(keep, norm[:, s] * sgt_ref[:, s] - rawt_ref[:, s] * coef[:, s], 0.0).astype(BF16)
        rgt_ref[:, s] = rg
        later_ref[j] = (jnp.zeros((DH, DH), F32) if whole is None else whole).astype(BF16)
        block = dot(qt_ref[:, s], rg, 1, 1)
        whole = block if whole is None else whole + block
    chunked(out_ref, whole, 0, parts)


def leaf_kernel(q_ref, km_ref, vm_ref, vt_ref, pt_ref, rgt_ref, states_ref, later_ref, rawt_ref, norm_ref, gain_ref, after_ref, lo_ref, qg_ref, kg_ref, vg_ref, done_ref):
    done_ref[...] = jnp.zeros_like(done_ref)
    rows = q_ref.shape[0]
    lo_ref[...] = ((rawt_ref[...] * norm_ref[...]).T * gain_ref[...].astype(F32)).astype(BF16)
    first = lax.broadcasted_iota(jnp.int32, (BLOCK, BLOCK), 0)
    second = lax.broadcasted_iota(jnp.int32, (BLOCK, BLOCK), 1)
    for j in range(rows // BLOCK):
        s = slice(j * BLOCK, (j + 1) * BLOCK)
        rgt = rgt_ref[:, s]
        rg = rgt.astype(F32).T.astype(BF16)
        dp = jnp.where(second <= first, dot(rg, vt_ref[:, s]), 0.0).astype(BF16)
        qg_ref[s, :] = (dot(rg, states_ref[j], 1, 1) + dot(dp, km_ref[s, :])).astype(BF16)
        dpt = jnp.where(first <= second, dot(vm_ref[s, :], rgt), 0.0).astype(BF16)
        kg_ref[s, :] = (dot(dpt, q_ref[s, :]) + dot(vm_ref[s, :], later_ref[j], 1, 1)).astype(BF16)
        vg_ref[s, :] = (dot(pt_ref[s, :], rg) + dot(km_ref[s, :], later_ref[j])).astype(BF16)


def by_branch_kernel(rows, in_ref, flags_ref, out_ref):
    zero = one = None
    for part in range(in_ref.shape[0]):
        value = in_ref[part]
        first = flags_ref[part, 2 * rows : 2 * rows + 1, :] == 0.0
        a = jnp.where(first, value, 0.0)
        b = jnp.where(first, 0.0, value)
        zero = a if zero is None else zero + a
        one = b if one is None else one + b
    out_ref[:rows] = zero
    out_ref[rows:] = one


def total_kernel(rows, members, own_ref, other_ref, after_ref, out_ref):
    zero = own_ref[:rows] + other_ref[:rows]
    one = own_ref[rows:] + other_ref[rows:]
    own = jnp.where(lax.axis_index("leaf") >= members, one, zero)
    both = zero + one
    for part in range(members):
        out_ref[part, :rows] = both
        out_ref[part, rows:] = own


def tree_kernel(rows, in_ref, tk_ref, tv_ref, bk_ref, bv_ref, tkg_hbm, tvg_hbm, bkg_hbm, bvg_hbm, tkg_ref, tvg_ref, bkg_ref, bvg_ref, sems):
    copies = [
        pltpu.make_async_copy(source, target, sems.at[i])
        for i, (source, target) in enumerate(
            ((tkg_ref, tkg_hbm), (tvg_ref, tvg_hbm), (bkg_ref, bkg_hbm), (bvg_ref, bvg_hbm))
        )
    ]
    for i, (start, k_ref, v_ref, kg_ref, vg_ref) in enumerate(
        ((0, tk_ref, tv_ref, tkg_ref, tvg_ref), (rows, bk_ref, bv_ref, bkg_ref, bvg_ref))
    ):
        grad = in_ref[:, start : start + rows, :].reshape(DH, DH)
        high = grad.astype(BF16)
        rest = grad - high.astype(F32)
        middle = rest.astype(BF16)
        low = (rest - middle.astype(F32)).astype(BF16)
        keys, values = k_ref[...], v_ref[...]
        twice = functools.partial(jnp.concatenate, axis=1)
        most = dot(twice([values, values]), twice([high, middle]), 1, 1)
        kg_ref[...] = (most + dot(values, low, 1, 1)).astype(BF16)
        copies[2 * i].start()
        most = dot(twice([keys, keys]), jnp.concatenate([high, middle], axis=0))
        vg_ref[...] = (most + dot(keys, low)).astype(BF16)
        copies[2 * i + 1].start()
    for copy in copies:
        copy.wait()


def led_by(members, lead):
    return [lead] + [i for i in members if i != lead]


def shards(mesh_shape, leaf_query, leaf_keys, leaf_values, out_grad, leaf_len, branch_id, trunk_keys, trunk_values, branch_keys, branch_values, norm_gain):
    leaves, heads = mesh_shape
    rows = leaf_query.shape[0]
    tree_rows = trunk_keys.shape[0]
    blocks = rows // BLOCK
    members = leaves // 2
    part = DH // members
    order = led_by(range(members), LEAD)
    halves = [[h * members + i for i in order] for h in range(2)]
    wide_x, wide_y = 4, 8
    plane = wide_x * wide_y
    y_order = led_by(range(wide_y), 0)
    xz_order = led_by([z + x for z in range(0, heads, plane) for x in range(wide_x)], heads - plane)
    y_groups = [[z + y * wide_x + x for y in y_order] for z in range(0, heads, plane) for x in range(wide_x)]
    xz_groups = [[i + y * wide_x for i in xz_order] for y in range(wide_y)]
    across = [(i, i ^ members) for i in range(leaves)]
    gain = norm_gain.reshape(1, DH)

    def exchange(value, axis, groups):
        return lax.all_to_all(value, axis, 0, 0, tiled=True, axis_index_groups=groups)

    held = pltpu.VMEM((tree_rows, DH), BF16)
    stay = functools.partial(pltpu.with_memory_space_constraint, memory_space=pltpu.MemorySpace.HBM)
    (sent,) = call(
        functools.partial(state_kernel, members),
        "state",
        [((members, 2 * part + 8, DH), F32)],
        [SM] + [HB] * 4,
        scratch=[held] * 4 + [pltpu.SemaphoreType.DMA((4,))],
    )(branch_id, *map(stay, (trunk_keys, trunk_values, branch_keys, branch_values)))
    got = exchange(sent, "leaf", halves)
    (half,) = call(functools.partial(half_sum_kernel, part), "half", [((2 * part, DH), F32)], [VM])(got)
    other = lax.ppermute(half, "leaf", across)
    qt, km, vm, vt, pt, lt, sgt, first = call(
        local_kernel,
        "local",
        [
            ((DH, rows), BF16),
            ((rows, DH), BF16),
            ((rows, DH), BF16),
            ((DH, rows), BF16),
            ((rows, BLOCK), BF16),
            ((DH, rows), F32),
            ((DH, rows), F32),
            ((blocks - 1, DH, DH), F32),
        ],
        [SM] + [VM] * 5 + [ANY],
        flops=1000,
        moved=1000,
    )(leaf_len, leaf_query, leaf_keys, leaf_values, out_grad, gain, half)
    (chunk,) = call(
        functools.partial(prefix_kernel, part, members), "prefix", [((members, part, DH), F32)], [VM] * 3 + [ANY]
    )(half, other, got, first)
    state = exchange(chunk, "leaf", halves)
    states, rawt, sums = call(
        functools.partial(raw_kernel, wide_y),
        "raw",
        [((blocks, DH, DH), BF16), ((DH, rows), F32), ((wide_y, 2, rows), F32)],
        [SM] + [VM] * 5,
    )(leaf_len, state, first, qt, lt, sgt)
    sums = exchange(sums, "head", y_groups)
    (sums,) = call(spread_kernel, "spread", [((len(xz_groups[0]), 2, rows), F32)], [VM])(sums)
    sums = exchange(sums, "head", xz_groups)
    rgt, norm, later, sent = call(
        functools.partial(grad_kernel, heads * DH, members),
        "grad",
        [((DH, rows), BF16), ((1, rows), F32), ((blocks, DH, DH), BF16), ((members, part, DH), F32)],
        [SM] + [VM] * 4,
    )(leaf_len, sums, rawt, sgt, qt)
    parts = exchange(sent, "leaf", halves)
    leaf = ((rows, DH), BF16)
    (own,) = call(functools.partial(by_branch_kernel, part), "by_branch", [((2 * part, DH), F32)], [VM] * 2)(parts, got)
    other = lax.ppermute(own, "leaf", across)
    *leaf_grads, done = call(
        leaf_kernel, "leaf", [leaf] * 4 + [((8, DH), F32)], [VM] * 11 + [ANY], flops=8 * rows * BLOCK * DH, moved=6 * MIB
    )(leaf_query, km, vm, vt, pt, rgt, states, later, rawt, norm, gain, own)
    (sent,) = call(
        functools.partial(total_kernel, part, members), "total", [((members, 2 * part, DH), F32)], [VM] * 2 + [ANY]
    )(own, other, done)
    grads = exchange(sent, "leaf", halves)
    tree = ((tree_rows, DH), BF16)
    tree_grads = call(
        functools.partial(tree_kernel, part),
        "tree",
        [tree] * 4,
        [VM] * 5,
        out=[HB] * 4,
        scratch=[held] * 4 + [pltpu.SemaphoreType.DMA((4,))],
    )(grads, trunk_keys, trunk_values, branch_keys, branch_values)
    return (*leaf_grads, *tree_grads)


def solution(mesh):
    wide = P("leaf", "head")
    placed = (wide, wide, wide, wide, P("leaf"), P("leaf"), wide, wide, wide, wide, P("head"))
    return jax.shard_map(
        functools.partial(shards, (mesh.shape["leaf"], mesh.shape["head"])),
        mesh=mesh,
        in_specs=placed,
        out_specs=(wide,) * 8,
        check_vma=False,
    )
```
